32 devices in a mesh: groups: 2 (over x), tiles: 8 (over z, y), seg: 2 (over core).
Axes of the slice: x: 2, y: 2, z: 4, core: 2. Of those that a mesh axis runs over, the one named last changes fastest.
Arguments:
- records: bfloat16 [2, 12800, 2048], P('seg', 'tiles', 'groups'), parts along dimension 2, may hold values from -6 to 6
- channel_live: int32 [2048], P(('groups', 'tiles')), parts along dimension 0, may hold values 0 or 1
Outputs:
- cross_spectra: bfloat16 [2, 2048, 128, 256], P(None, ('groups', 'tiles'), None, 'seg'), parts along dimension 1
The draws below stay inside these ranges and needn't reach their ends.
There are 2 independent parts, one for each index of `groups`. The reference program is written for one: setup_inputs(seed, part) draws one part's arguments, and reference() takes and returns one part's arrays. A program takes and returns all parts, laid end to end along the dimension named above; each array names one. Nothing has to cross between parts.
All inputs are finite; a program needn't handle non-finite values. No bound on the sum of `channel_live` on one device may be relied on, other than what follows from the above.
Results may differ from the reference program's by a relative error of at most 0.0069.
Values may be sent and summed in bfloat16 or wider, within the bound.
A program may use at most 128 MiB of HBM per device.

```python
import math
import jax
import jax.numpy as jnp
from jax import lax

G = 128
OFFS = 128
L = 12800
FIRST_BIN = 64
F = 256
CHANNELS = 1024
WINDOWS = 2


def set_ends(values, own_key, least, top_value):
    extent = values.shape
    spot = [jax.random.randint(jax.random.fold_in(own_key, axis), (), 0, extent[axis]) for axis in range(len(extent))]
    values = values.at[tuple(spot)].set(least)
    longest = extent.index(max(extent))
    spot[longest] = (spot[longest] + 1) % extent[longest]
    return values.at[tuple(spot)].set(top_value)


def block_levels(own_key, extent, cuts, low, largest):
    factor_of, own = 1.0, jax.random.fold_in(own_key, 6)
    for dim, blocks in cuts:
        heights = jnp.exp(jax.random.uniform(jax.random.fold_in(own, dim), (blocks,), jnp.float32, low / len(cuts), largest / len(cuts)))
        factor_of = factor_of * jnp.repeat(heights, extent[dim] // blocks).reshape([-1 if axis == dim else 1 for axis in range(len(extent))])
    return factor_of


def bell_draw(stream_key, extent, width, limit, shards=(), kind=jnp.bfloat16):
    level = block_levels(stream_key, extent, shards, -0.22, 0.18) if shards else 1.0
    entries = jax.random.normal(stream_key, extent, jnp.float32) * width * level
    return jnp.minimum(jnp.maximum(entries, -limit), limit).astype(kind)


def setup_inputs(seed: int = 0, part: int = 0) -> dict:
    arg_keys = jax.random.split(jax.random.key(seed), 3)
    part_splits = jax.random.split(jax.random.fold_in(arg_keys[2], part), 3)
    return {
        "records": bell_draw(part_splits[0], (WINDOWS, L, CHANNELS), 1.0, 6.0, ((0, 2), (1, 8))),
        "channel_live": set_ends((jax.random.randint(part_splits[1], (CHANNELS,), 0, 8) < 7).astype(jnp.int32), jax.random.fold_in(part_splits[1], 1), 0, 1),
    }


epsilon = 1e-06

def band_table(length, first_bin, bin_count):
    sample = jnp.arange(length, dtype=jnp.int32)[:, None]
    bin_index = jnp.arange(bin_count, dtype=jnp.int32)[None, :] + first_bin
    phase_index = sample * bin_index % length
    phase_angle = phase_index.astype(jnp.float32) * (2.0 * math.pi / length)
    hann_taper = 0.5 - 0.5 * jnp.cos(sample.astype(jnp.float32) * (2.0 * math.pi / length))
    return jnp.concatenate([hann_taper * jnp.cos(phase_angle), -hann_taper * jnp.sin(phase_angle)], axis=1).astype(jnp.bfloat16)

def whiten(spectra, live_mask):
    mean_power = lax.optimization_barrier(jnp.mean(spectra * spectra, axis=2, keepdims=True))
    gains = lax.rsqrt(mean_power + epsilon) * live_mask.astype(jnp.float32)[None, :, None]
    return (spectra * gains).astype(jnp.bfloat16)

def cross_band(own_real, own_imag, next_real, next_imag, offsets):
    group_size = own_real.shape[1]
    wide_real = jnp.concatenate([own_real, next_real], axis=1)
    wide_imag = jnp.concatenate([own_imag, next_imag], axis=1)
    moved_real = jnp.stack([wide_real[:, offset:offset + group_size] for offset in range(offsets)], axis=2).astype(jnp.float32)
    moved_imag = jnp.stack([wide_imag[:, offset:offset + group_size] for offset in range(offsets)], axis=2).astype(jnp.float32)
    base_real = own_real.astype(jnp.float32)[:, :, None, :]
    base_imag = own_imag.astype(jnp.float32)[:, :, None, :]
    real_sum = lax.optimization_barrier(jnp.sum(base_real * moved_real + base_imag * moved_imag, axis=0))
    imag_sum = lax.optimization_barrier(jnp.sum(base_imag * moved_real - base_real * moved_imag, axis=0))
    return jnp.stack([real_sum, imag_sum])

def reference(records, channel_live):
    basis_table = band_table(L, FIRST_BIN, F).astype(jnp.float32)

    def transform(window):
        return jnp.dot(jnp.transpose(window).astype(jnp.float32), basis_table, precision=lax.Precision.HIGHEST)
    spectra = lax.map(transform, records)
    whitened = whiten(spectra, channel_live)
    real_part = whitened[..., :F]
    imag_part = whitened[..., F:]
    windows = real_part.shape[0]
    padding = jnp.zeros((windows, G, F), jnp.bfloat16)
    real_padded = jnp.concatenate([real_part, padding], axis=1)
    imag_padded = jnp.concatenate([imag_part, padding], axis=1)
    group_count = real_part.shape[1] // G

    def one_group(group_index):
        first_row = (group_index * G).astype(jnp.int32)
        own_real = lax.dynamic_slice_in_dim(real_padded, first_row, G, 1)
        own_imag = lax.dynamic_slice_in_dim(imag_padded, first_row, G, 1)
        next_real = lax.dynamic_slice_in_dim(real_padded, first_row + G, G, 1)
        next_imag = lax.dynamic_slice_in_dim(imag_padded, first_row + G, G, 1)
        stacked = cross_band(own_real, own_imag, next_real, next_imag, OFFS)
        return (stacked / windows).astype(jnp.bfloat16)
    blocks = lax.map(one_group, jnp.arange(group_count, dtype=jnp.int32))
    return jnp.transpose(blocks, (1, 0, 2, 3, 4)).reshape(2, group_count * G, OFFS, F)
```

```python
import functools
import math

import jax
import jax.numpy as jnp
import ml_dtypes
import numpy as np
from jax import lax
from jax.experimental import pallas as pl
from jax.experimental.pallas import tpu as pltpu
from jax.sharding import PartitionSpec as P

OFFS = 128
L = 12800
FIRST_BIN = 64
F = 256
MODES = 64
EPSILON = 1e-06
MESH = pl.DeviceIdType.MESH


def sequences(length):
    n = np.arange(length, dtype=np.float64)
    diagonal = ((length - 1 - 2 * n) / 2) ** 2 * np.cos(2 * np.pi * F / 2 / L)
    beside = n[1:] * (length - n[1:]) / 2
    matrix = np.diag(diagonal) + np.diag(beside, 1) + np.diag(beside, -1)
    rows = np.linalg.eigh(matrix)[1][:, ::-1][:, :MODES].T
    sign = np.sign(np.sum(rows * (1.0 + n / length + np.sin(n)), axis=1, keepdims=True))
    return rows * sign


def tables(tiles, length):
    rows = sequences(length)
    n = np.arange(length, dtype=np.float64) - (length - 1) / 2
    middle = FIRST_BIN + (F - 1) / 2
    turn = 2 * np.pi * middle * n / L
    taper = 0.5 - 0.5 * np.cos(2 * np.pi * np.arange(tiles * length) / L).reshape(tiles, 1, length)
    modulated = np.concatenate([rows * np.cos(turn), -rows * np.sin(turn)])
    analysis = (taper * modulated).astype(ml_dtypes.bfloat16)
    bins = np.arange(F, dtype=np.float64)
    spectrum = np.exp(-2j * np.pi * (bins[:, None] - (F - 1) / 2) * n / L) @ rows.T
    centre = np.arange(tiles) * length + (length - 1) / 2
    spectrum = spectrum * np.exp(-2j * np.pi * (bins + FIRST_BIN)[:, None] * centre[:, None, None] / L)
    re, im = spectrum.real, spectrum.imag
    whole = np.concatenate(
        [np.concatenate([re, -im], axis=2), np.concatenate([im, re], axis=2)], axis=1
    )
    high = whole.astype(ml_dtypes.bfloat16)
    low = (whole - high.astype(np.float64)).astype(ml_dtypes.bfloat16)
    return analysis, np.concatenate([high, low], axis=2)


def spectra_kernel(
    tiles, rec, analysis, synthesis, live, out,
    rec_buf, a_buf, s_buf, send_buf, recv_buf, total, y_buf, wide,
    rec_sem, a_sem, s_sem, send_sem, recv_sem, y_send, y_recv,
):
    t, s = lax.axis_index("tiles"), lax.axis_index("seg")
    half = F // 2
    group = live.shape[1]

    def fetch(j):
        j = pl.multiple_of(j * group, group)
        return j

    def rec_copy(j):
        return pltpu.make_async_copy(rec.at[0, :, pl.ds(fetch(j), group)], rec_buf.at[j], rec_sem.at[j])

    a_copy = pltpu.make_async_copy(analysis.at[t], a_buf, a_sem)
    a_copy.start()

    @pl.loop(1, tiles + 1)
    def _(i):
        rec_copy(lax.rem(t + i, tiles)).start()

    s_copy = pltpu.make_async_copy(synthesis, s_buf, s_sem)
    s_copy.start()

    barrier = pltpu.get_barrier_semaphore()

    @pl.loop(1, tiles)
    def _(i):
        pl.semaphore_signal(barrier, inc=1, device_id={"tiles": lax.rem(t + i, tiles)}, device_id_type=MESH)

    for step in (0, 1, tiles - 1):
        pl.semaphore_signal(
            barrier, inc=1, device_id={"tiles": lax.rem(t + step, tiles), "seg": 1 - s}, device_id_type=MESH
        )

    def coefficients(j):
        rec_copy(j).wait()
        return jnp.dot(a_buf[...], rec_buf[j], preferred_element_type=jnp.float32).astype(jnp.bfloat16)

    def send(j):
        return pltpu.make_async_remote_copy(
            src_ref=send_buf.at[j], dst_ref=recv_buf.at[t], send_sem=send_sem.at[j], recv_sem=recv_sem.at[t],
            device_id={"tiles": j}, device_id_type=MESH,
        )

    a_copy.wait()
    first = lax.rem(t + 1, tiles)
    send_buf[first] = coefficients(first)
    pl.semaphore_wait(barrier, tiles + 2)
    send(first).start()

    @pl.loop(2, tiles)
    def _(i):
        j = lax.rem(t + i, tiles)
        send_buf[j] = coefficients(j)
        send(j).start()

    def part(i, own):
        both = jnp.concatenate([own, own], axis=0)
        return jnp.dot(s_buf[i], both, preferred_element_type=jnp.float32)

    own = coefficients(t)
    s_copy.wait()
    total[...] = part(t, own)

    @pl.loop(1, tiles)
    def _(i):
        j = lax.rem(t + tiles - i, tiles)
        pltpu.make_async_remote_copy(
            src_ref=send_buf.at[j], dst_ref=recv_buf.at[j], send_sem=send_sem.at[j], recv_sem=recv_sem.at[j],
            device_id={"tiles": j}, device_id_type=MESH,
        ).wait_recv()
        total[...] += part(j, recv_buf[j])

    spectra = total[...]
    power = jnp.sum(spectra * spectra, axis=0, keepdims=True) * (1.0 / (2 * F))
    gains = lax.rsqrt(power + EPSILON) * live[...].astype(jnp.float32)
    whitened = jnp.transpose(spectra * gains).astype(jnp.bfloat16)
    for p in range(2):
        for q in range(2):
            y_buf[p, q] = whitened[:, q * F + p * half:q * F + (p + 1) * half]

    across = pltpu.make_async_remote_copy(
        src_ref=y_buf.at[1 - s], dst_ref=wide.at[0, s], send_sem=y_send.at[0], recv_sem=y_recv.at[0],
        device_id={"seg": 1 - s}, device_id_type=MESH,
    )
    before = lax.rem(t + tiles - 1, tiles)
    back_same = pltpu.make_async_remote_copy(
        src_ref=y_buf.at[s], dst_ref=wide.at[1, s], send_sem=y_send.at[1], recv_sem=y_recv.at[1],
        device_id={"tiles": before}, device_id_type=MESH,
    )
    back_other = pltpu.make_async_remote_copy(
        src_ref=y_buf.at[1 - s], dst_ref=wide.at[1, s], send_sem=y_send.at[2], recv_sem=y_recv.at[2],
        device_id={"tiles": before, "seg": 1 - s}, device_id_type=MESH,
    )

    @pl.when(t > 0)
    def _():
        back_same.start()
        back_other.start()

    across.start()
    rows = pl.ds(0, group)
    next_rows = pl.ds(group, group)
    out[s, :, rows, :] = y_buf[s].astype(jnp.float32)

    @pl.loop(1, tiles)
    def _(i):
        send(lax.rem(t + i, tiles)).wait_send()

    across.wait_recv()
    out[1 - s, :, rows, :] = wide[0, 1 - s].astype(jnp.float32)

    @pl.when(t < tiles - 1)
    def _():
        back_same.wait_recv()
        pltpu.make_async_remote_copy(
            src_ref=y_buf.at[1 - s], dst_ref=wide.at[1, 1 - s], send_sem=y_send.at[2], recv_sem=y_recv.at[2],
            device_id={"tiles": before, "seg": 1 - s}, device_id_type=MESH,
        ).wait_recv()
        out[:, :, next_rows, :] = wide[1].astype(jnp.float32)

    @pl.when(t == tiles - 1)
    def _():
        out[:, :, next_rows, :] = jnp.zeros((2, 2, group, half), jnp.float32)

    @pl.when(t > 0)
    def _():
        back_same.wait_send()
        back_other.wait_send()

    across.wait_send()


def whitened_spectra(records, channel_live, tiles):
    length = records.shape[1]
    group = channel_live.shape[0]
    half = F // 2
    analysis, synthesis = tables(tiles, length)
    anywhere = pl.BlockSpec(memory_space=pl.ANY)
    vmem = pl.BlockSpec(memory_space=pltpu.VMEM)
    return pl.pallas_call(
        functools.partial(spectra_kernel, tiles),
        out_shape=jax.ShapeDtypeStruct((2, 2, 2 * group, half), jnp.float32),
        in_specs=[anywhere, anywhere, anywhere, vmem],
        out_specs=vmem,
        scratch_shapes=[
            pltpu.VMEM((tiles, length, group), jnp.bfloat16),
            pltpu.VMEM((2 * MODES, length), jnp.bfloat16),
            pltpu.VMEM((tiles, 2 * F, 4 * MODES), jnp.bfloat16),
            pltpu.VMEM((tiles, 2 * MODES, group), jnp.bfloat16),
            pltpu.VMEM((tiles, 2 * MODES, group), jnp.bfloat16),
            pltpu.VMEM((2 * F, group), jnp.float32),
            pltpu.VMEM((2, 2, group, half), jnp.bfloat16),
            pltpu.VMEM((2, 2, 2, group, half), jnp.bfloat16),
            pltpu.SemaphoreType.DMA((tiles,)),
            pltpu.SemaphoreType.DMA,
            pltpu.SemaphoreType.DMA,
            pltpu.SemaphoreType.DMA((tiles,)),
            pltpu.SemaphoreType.DMA((tiles,)),
            pltpu.SemaphoreType.DMA((3,)),
            pltpu.SemaphoreType.DMA((3,)),
        ],
        compiler_params=pltpu.CompilerParams(
            collective_id=0, has_side_effects=True, vmem_limit_bytes=40 << 20
        ),
    )(records, jnp.asarray(analysis), jnp.asarray(synthesis), channel_live.reshape(1, group))


CHANNEL_BLOCK = 8
OFFSET_BLOCK = 32


def cross_kernel(scale, wide, out):
    first = pl.program_id(0) * CHANNEL_BLOCK

    @pl.loop(0, CHANNEL_BLOCK)
    def _(i):
        c = first + i
        base = [[wide[w, q, pl.ds(c, 1), :] * scale for q in range(2)] for w in range(2)]
        for o in range(0, OFFS, OFFSET_BLOCK):
            real, imag = None, None
            for w in range(2):
                re, im = base[w]
                moved_re = wide[w, 0, pl.ds(c + o, OFFSET_BLOCK), :]
                moved_im = wide[w, 1, pl.ds(c + o, OFFSET_BLOCK), :]
                more_real = re * moved_re + im * moved_im
                more_imag = im * moved_re - re * moved_im
                real = more_real if real is None else real + more_real
                imag = more_imag if imag is None else imag + more_imag
            out[0, i, pl.ds(o, OFFSET_BLOCK), :] = real.astype(jnp.bfloat16)
            out[1, i, pl.ds(o, OFFSET_BLOCK), :] = imag.astype(jnp.bfloat16)


def cross_spectra(wide, windows):
    group, half = wide.shape[2] // 2, wide.shape[3]
    return pl.pallas_call(
        functools.partial(cross_kernel, 1.0 / windows),
        grid=(group // CHANNEL_BLOCK,),
        out_shape=jax.ShapeDtypeStruct((2, group, OFFS, half), jnp.bfloat16),
        in_specs=[pl.BlockSpec(memory_space=pltpu.VMEM)],
        out_specs=pl.BlockSpec((2, CHANNEL_BLOCK, OFFS, half), lambda i: (0, i, 0, 0)),
        compiler_params=pltpu.CompilerParams(vmem_limit_bytes=16 << 20),
    )(wide)


def solution(mesh):
    tiles = mesh.shape["tiles"]

    def local(records, channel_live):
        wide = whitened_spectra(records, channel_live, tiles)
        return cross_spectra(wide, records.shape[0] * mesh.shape["seg"])

    in_specs = (P("seg", "tiles", "groups"), P(("groups", "tiles")))
    out_specs = P(None, ("groups", "tiles"), None, "seg")
    return jax.shard_map(local, mesh=mesh, in_specs=in_specs, out_specs=out_specs, check_vma=False)
```

```python
import functools
import math

import jax
import jax.numpy as jnp
import ml_dtypes
import numpy as np
from jax import lax
from jax.experimental import pallas as pl
from jax.experimental.pallas import tpu as pltpu
from jax.sharding import PartitionSpec as P

OFFS = 128
L = 12800
FIRST_BIN = 64
F = 256
MODES = 64
EPSILON = 1e-06
MESH = pl.DeviceIdType.MESH


def sequences(length):
    n = np.arange(length, dtype=np.float64)
    diagonal = ((length - 1 - 2 * n) / 2) ** 2 * np.cos(2 * np.pi * F / 2 / L)
    beside = n[1:] * (length - n[1:]) / 2
    matrix = np.diag(diagonal) + np.diag(beside, 1) + np.diag(beside, -1)
    rows = np.linalg.eigh(matrix)[1][:, ::-1][:, :MODES].T
    sign = np.sign(np.sum(rows * (1.0 + n / length + np.sin(n)), axis=1, keepdims=True))
    return rows * sign


def tables(tiles, length):
    rows = sequences(length)
    n = np.arange(length, dtype=np.float64) - (length - 1) / 2
    middle = FIRST_BIN + (F - 1) / 2
    turn = 2 * np.pi * middle * n / L
    taper = 0.5 - 0.5 * np.cos(2 * np.pi * np.arange(tiles * length) / L).reshape(tiles, length)
    modulated = np.concatenate([rows * np.cos(turn), -rows * np.sin(turn)])
    analysis = (np.round(np.concatenate([modulated, taper]) * 2.0**20) / 2.0**20).astype(np.float32)
    bins = np.arange(F, dtype=np.float64)
    spectrum = np.exp(-2j * np.pi * (bins[:, None] - (F - 1) / 2) * n / L) @ rows.T
    centre = np.arange(tiles) * length + (length - 1) / 2
    spectrum = spectrum * np.exp(-2j * np.pi * (bins + FIRST_BIN)[:, None] * centre[:, None, None] / L)
    re, im = spectrum.real, spectrum.imag
    whole = np.concatenate(
        [np.concatenate([re, -im], axis=2), np.concatenate([im, re], axis=2)], axis=1
    )
    high = whole.astype(ml_dtypes.bfloat16)
    low = (whole - high.astype(np.float64)).astype(ml_dtypes.bfloat16)
    return analysis, np.concatenate([high, low], axis=2)


def spectra_kernel(
    tiles, rec, analysis, synthesis, live, out,
    rec_buf, table, a_buf, s_buf, live_buf, send_buf, recv_buf, total, y_buf, blank,
    rec_sem, a_sem, s_sem, live_sem, out_sem, send_sem, recv_sem, y_send, y_recv,
):
    t, s = lax.axis_index("tiles"), lax.axis_index("seg")
    half = F // 2
    group = live.shape[1]

    def rec_copy(j):
        columns = pl.ds(pl.multiple_of(j * group, group), group)
        return pltpu.make_async_copy(rec.at[0, :, columns], rec_buf.at[j], rec_sem.at[j])

    a_copy = pltpu.make_async_copy(analysis, table, a_sem)
    a_copy.start()

    @pl.loop(1, tiles + 1)
    def _(i):
        rec_copy(lax.rem(t + i, tiles)).start()

    s_copy = pltpu.make_async_copy(synthesis, s_buf, s_sem)
    s_copy.start()
    live_copy = pltpu.make_async_copy(live, live_buf, live_sem)
    live_copy.start()

    barrier = pltpu.get_barrier_semaphore()

    @pl.loop(1, tiles)
    def _(i):
        pl.semaphore_signal(barrier, inc=1, device_id={"tiles": lax.rem(t + i, tiles)}, device_id_type=MESH)

    for step in (0, 1, tiles - 1):
        pl.semaphore_signal(
            barrier, inc=1, device_id={"tiles": lax.rem(t + step, tiles), "seg": 1 - s}, device_id_type=MESH
        )

    def coefficients(j):
        rec_copy(j).wait()
        return jnp.dot(a_buf[...], rec_buf[j], preferred_element_type=jnp.float32).astype(jnp.bfloat16)

    def send(j):
        return pltpu.make_async_remote_copy(
            src_ref=send_buf.at[j], dst_ref=recv_buf.at[t], send_sem=send_sem.at[j], recv_sem=recv_sem.at[t],
            device_id={"tiles": j}, device_id_type=MESH,
        )

    a_copy.wait()
    taper = table[pl.ds(2 * MODES + t, 1), :]
    a_buf[...] = (table[pl.ds(0, 2 * MODES), :] * taper).astype(jnp.bfloat16)
    first = lax.rem(t + 1, tiles)
    send_buf[first] = coefficients(first)
    pl.semaphore_wait(barrier, tiles + 2)
    send(first).start()

    @pl.loop(2, tiles)
    def _(i):
        j = lax.rem(t + i, tiles)
        send_buf[j] = coefficients(j)
        send(j).start()

    def part(i, own):
        both = jnp.concatenate([own, own], axis=0)
        return jnp.dot(s_buf[i], both, preferred_element_type=jnp.float32)

    own = coefficients(t)
    s_copy.wait()
    total[...] = part(t, own)

    @pl.loop(1, tiles)
    def _(i):
        j = lax.rem(t + tiles - i, tiles)
        pltpu.make_async_remote_copy(
            src_ref=send_buf.at[j], dst_ref=recv_buf.at[j], send_sem=send_sem.at[j], recv_sem=recv_sem.at[j],
            device_id={"tiles": j}, device_id_type=MESH,
        ).wait_recv()
        total[...] += part(j, recv_buf[j])

    live_copy.wait()
    spectra = total[...]
    power = jnp.sum(spectra * spectra, axis=0, keepdims=True) * (1.0 / (2 * F))
    gains = lax.rsqrt(power + EPSILON) * live_buf[...].astype(jnp.float32)
    whitened = jnp.transpose(spectra * gains).astype(jnp.bfloat16)
    for p in range(2):
        for q in range(2):
            y_buf[p, q] = whitened[:, q * F + p * half:q * F + (p + 1) * half]

    before = lax.rem(t + tiles - 1, tiles)

    def hand_over(bins, place, window, k, **device):
        return pltpu.make_async_remote_copy(
            src_ref=y_buf.at[bins], dst_ref=out.at[place, window], send_sem=y_send.at[k], recv_sem=y_recv.at[k],
            device_id=device, device_id_type=MESH,
        )

    back_same = hand_over(s, 1, s, 1, tiles=before)
    back_other = hand_over(1 - s, 1, s, 2, tiles=before, seg=1 - s)
    across = hand_over(1 - s, 0, s, 0, seg=1 - s)

    @pl.when(t > 0)
    def _():
        back_same.start()
        back_other.start()

    across.start()
    keep = pltpu.make_async_copy(y_buf.at[s], out.at[0, s], out_sem.at[0])
    keep.start()

    @pl.when(t == tiles - 1)
    def _():
        blank[...] = jnp.zeros_like(blank)
        clear = pltpu.make_async_copy(blank, out.at[1], out_sem.at[1])
        clear.start()
        clear.wait()

    @pl.loop(1, tiles)
    def _(i):
        send(lax.rem(t + i, tiles)).wait_send()

    keep.wait()
    hand_over(1 - s, 0, 1 - s, 0, seg=1 - s).wait_recv()

    @pl.when(t < tiles - 1)
    def _():
        back_same.wait_recv()
        hand_over(1 - s, 1, 1 - s, 2, tiles=before, seg=1 - s).wait_recv()

    @pl.when(t > 0)
    def _():
        back_same.wait_send()
        back_other.wait_send()

    across.wait_send()


def whitened_spectra(records, channel_live, tiles):
    length = records.shape[1]
    group = channel_live.shape[0]
    half = F // 2
    analysis, synthesis = tables(tiles, length)
    in_hbm = pl.BlockSpec(memory_space=pltpu.HBM)
    return pl.pallas_call(
        functools.partial(spectra_kernel, tiles),
        out_shape=jax.ShapeDtypeStruct((2, 2, 2, group, half), jnp.bfloat16),
        in_specs=[in_hbm] * 4,
        out_specs=in_hbm,
        scratch_shapes=[
            pltpu.VMEM((tiles, length, group), jnp.bfloat16),
            pltpu.VMEM((2 * MODES + tiles, length), jnp.float32),
            pltpu.VMEM((2 * MODES, length), jnp.bfloat16),
            pltpu.VMEM((tiles, 2 * F, 4 * MODES), jnp.bfloat16),
            pltpu.VMEM((1, group), jnp.int32),
            pltpu.VMEM((tiles, 2 * MODES, group), jnp.bfloat16),
            pltpu.VMEM((tiles, 2 * MODES, group), jnp.bfloat16),
            pltpu.VMEM((2 * F, group), jnp.float32),
            pltpu.VMEM((2, 2, group, half), jnp.bfloat16),
            pltpu.VMEM((2, 2, group, half), jnp.bfloat16),
            pltpu.SemaphoreType.DMA((tiles,)),
            pltpu.SemaphoreType.DMA,
            pltpu.SemaphoreType.DMA,
            pltpu.SemaphoreType.DMA,
            pltpu.SemaphoreType.DMA((2,)),
            pltpu.SemaphoreType.DMA((tiles,)),
            pltpu.SemaphoreType.DMA((tiles,)),
            pltpu.SemaphoreType.DMA((3,)),
            pltpu.SemaphoreType.DMA((3,)),
        ],
        compiler_params=pltpu.CompilerParams(
            collective_id=0, has_side_effects=True, vmem_limit_bytes=60 << 20
        ),
    )(records, jnp.asarray(analysis), jnp.asarray(synthesis), channel_live.reshape(1, group))


CHANNEL_BLOCK = 8
OFFSET_BLOCK = 32


def cross_kernel(scale, halves, out, wide, stack, sem):
    group = halves.shape[3]
    for w in range(2):
        for place in range(2):
            re, im = (halves[place, w, q].astype(jnp.float32) for q in range(2))
            rows = pl.ds(place * group, group)
            wide[w, 0, rows, :] = re
            wide[w, 1, rows, :] = im
            wide[w, 2, rows, :] = re + im

    def channel(c):
        (a0, b0), (a1, b1) = [[wide[w, q, pl.ds(c, 1), :] * scale for q in range(2)] for w in range(2)]
        pairs = ((2, b0, b1), (0, a0 - b0, a1 - b1), (1, a0 + b0, a1 + b1))
        for o in range(0, OFFS, OFFSET_BLOCK):
            rows = pl.ds(c + o, OFFSET_BLOCK)
            shared, more, less = (
                first * wide[0, q, rows, :] + second * wide[1, q, rows, :] for q, first, second in pairs
            )
            stack[0, c, pl.ds(o, OFFSET_BLOCK), :] = (shared + more).astype(jnp.bfloat16)
            stack[1, c, pl.ds(o, OFFSET_BLOCK), :] = (shared - less).astype(jnp.bfloat16)

    def copies(k):
        rows = pl.ds(k * CHANNEL_BLOCK, CHANNEL_BLOCK)
        return [pltpu.make_async_copy(stack.at[q, rows], out.at[q, rows], sem.at[q, k]) for q in range(2)]

    @pl.loop(0, group // CHANNEL_BLOCK)
    def _(k):
        for i in range(CHANNEL_BLOCK):
            channel(k * CHANNEL_BLOCK + i)
        for copy in copies(k):
            copy.start()

    @pl.loop(0, group // CHANNEL_BLOCK)
    def _(k):
        for copy in copies(k):
            copy.wait()


def cross_spectra(halves, windows):
    group, half = halves.shape[3:]
    return pl.pallas_call(
        functools.partial(cross_kernel, 1.0 / windows),
        out_shape=jax.ShapeDtypeStruct((2, group, OFFS, half), jnp.bfloat16),
        in_specs=[pl.BlockSpec(memory_space=pltpu.VMEM)],
        out_specs=pl.BlockSpec(memory_space=pltpu.HBM),
        scratch_shapes=[
            pltpu.VMEM((2, 3, 2 * group, half), jnp.float32),
            pltpu.VMEM((2, group, OFFS, half), jnp.bfloat16),
            pltpu.SemaphoreType.DMA((2, group // CHANNEL_BLOCK)),
        ],
        compiler_params=pltpu.CompilerParams(vmem_limit_bytes=60 << 20),
    )(halves)


def solution(mesh):
    tiles = mesh.shape["tiles"]

    def local(records, channel_live):
        halves = whitened_spectra(records, channel_live, tiles)
        return cross_spectra(halves, records.shape[0] * mesh.shape["seg"])

    in_specs = (P("seg", "tiles", "groups"), P(("groups", "tiles")))
    out_specs = P(None, ("groups", "tiles"), None, "seg")
    return jax.shard_map(local, mesh=mesh, in_specs=in_specs, out_specs=out_specs, check_vma=False)
```

```python
import functools
import math

import jax
import jax.numpy as jnp
import ml_dtypes
import numpy as np
from jax import lax
from jax.experimental import pallas as pl
from jax.experimental.pallas import tpu as pltpu
from jax.sharding import PartitionSpec as P

OFFS = 128
L = 12800
FIRST_BIN = 64
F = 256
MODES = 48
EPSILON = 1e-06
MESH = pl.DeviceIdType.MESH


def sequences(length):
    n = np.arange(length, dtype=np.float64)
    diagonal = ((length - 1 - 2 * n) / 2) ** 2 * np.cos(2 * np.pi * F / 2 / L)
    beside = n[1:] * (length - n[1:]) / 2
    matrix = np.diag(diagonal) + np.diag(beside, 1) + np.diag(beside, -1)
    rows = np.linalg.eigh(matrix)[1][:, ::-1][:, :MODES].T
    sign = np.sign(np.sum(rows * (1.0 + n / length + np.sin(n)), axis=1, keepdims=True))
    return rows * sign


def tables(tiles, length):
    rows = sequences(length)
    n = np.arange(length, dtype=np.float64) - (length - 1) / 2
    middle = FIRST_BIN + (F - 1) / 2
    turn = 2 * np.pi * middle * n / L
    taper = 0.5 - 0.5 * np.cos(2 * np.pi * np.arange(tiles * length) / L).reshape(tiles, length)
    modulated = np.concatenate([rows * np.cos(turn), -rows * np.sin(turn)])
    analysis = (np.round(np.concatenate([modulated, taper]) * 2.0**20) / 2.0**20).astype(np.float32)
    bins = np.arange(F, dtype=np.float64)
    spectrum = np.exp(-2j * np.pi * (bins[:, None] - (F - 1) / 2) * n / L) @ rows.T
    centre = np.arange(tiles) * length + (length - 1) / 2
    spectrum = spectrum * np.exp(-2j * np.pi * (bins + FIRST_BIN)[:, None] * centre[:, None, None] / L)
    re, im = spectrum.real, spectrum.imag
    whole = np.concatenate(
        [np.concatenate([re, -im], axis=2), np.concatenate([im, re], axis=2)], axis=1
    )
    pairs = np.concatenate([whole[0::2], whole[1::2]], axis=2)
    return analysis, pairs.astype(ml_dtypes.bfloat16)


def spectra_kernel(
    tiles, rec, analysis, synthesis, live, out,
    rec_buf, table, a_buf, s_buf, live_buf, send_buf, recv_buf, total, y_buf, blank,
    rec_sem, a_sem, s_sem, live_sem, out_sem, send_sem, recv_sem, y_send, y_recv,
):
    t, s = lax.axis_index("tiles"), lax.axis_index("seg")
    half = F // 2
    group = live.shape[1]

    def rec_copy(j):
        columns = pl.ds(pl.multiple_of(j * group, group), group)
        return pltpu.make_async_copy(rec.at[0, :, columns], rec_buf.at[j], rec_sem.at[j])

    a_copy = pltpu.make_async_copy(analysis, table, a_sem)
    a_copy.start()

    @pl.loop(1, tiles + 1)
    def _(i):
        rec_copy(lax.rem(t + i, tiles)).start()

    s_copy = pltpu.make_async_copy(synthesis, s_buf, s_sem)
    s_copy.start()
    live_copy = pltpu.make_async_copy(live, live_buf, live_sem)
    live_copy.start()

    barrier = pltpu.get_barrier_semaphore()

    @pl.loop(1, tiles)
    def _(i):
        pl.semaphore_signal(barrier, inc=1, device_id={"tiles": lax.rem(t + i, tiles)}, device_id_type=MESH)

    for step in (0, 1, tiles - 1):
        pl.semaphore_signal(
            barrier, inc=1, device_id={"tiles": lax.rem(t + step, tiles), "seg": 1 - s}, device_id_type=MESH
        )

    def coefficients(j):
        rec_copy(j).wait()
        return jnp.dot(a_buf[...], rec_buf[j], preferred_element_type=jnp.float32).astype(jnp.bfloat16)

    def rows_of(j):
        return pl.ds(pl.multiple_of(j * 2 * MODES, 2 * MODES), 2 * MODES)

    def send(j):
        return pltpu.make_async_remote_copy(
            src_ref=send_buf.at[j], dst_ref=recv_buf.at[rows_of(t)], send_sem=send_sem.at[j],
            recv_sem=recv_sem.at[t], device_id={"tiles": j}, device_id_type=MESH,
        )

    def arrived(j):
        return pltpu.make_async_remote_copy(
            src_ref=send_buf.at[j], dst_ref=recv_buf.at[rows_of(j)], send_sem=send_sem.at[j],
            recv_sem=recv_sem.at[j], device_id={"tiles": j}, device_id_type=MESH,
        )

    a_copy.wait()
    taper = table[pl.ds(2 * MODES + t, 1), :]
    a_buf[...] = (table[pl.ds(0, 2 * MODES), :] * taper).astype(jnp.bfloat16)
    first = lax.rem(t + 1, tiles)
    send_buf[first] = coefficients(first)
    pl.semaphore_wait(barrier, tiles + 2)
    send(first).start()

    @pl.loop(2, tiles)
    def _(i):
        j = lax.rem(t + i, tiles)
        send_buf[j] = coefficients(j)
        send(j).start()

    recv_buf[rows_of(t), :] = coefficients(t)
    s_copy.wait()

    def part(p):
        rows = pl.ds(pl.multiple_of(p * 4 * MODES, 4 * MODES), 4 * MODES)
        return jnp.dot(s_buf[p], recv_buf[rows, :], preferred_element_type=jnp.float32)

    pair, pairs = lax.div(t, 2), tiles // 2
    arrived(pair * 2 + 1 - lax.rem(t, 2)).wait_recv()
    total[...] = part(pair)

    @pl.loop(1, pairs)
    def _(i):
        p = lax.rem(pair + pairs - i, pairs)
        arrived(2 * p).wait_recv()
        arrived(2 * p + 1).wait_recv()
        total[...] += part(p)

    live_copy.wait()
    spectra = total[...]
    power = jnp.sum(spectra * spectra, axis=0, keepdims=True) * (1.0 / (2 * F))
    gains = lax.rsqrt(power + EPSILON) * live_buf[...].astype(jnp.float32)
    before = lax.rem(t + tiles - 1, tiles)

    def hand_back(p, window):
        return pltpu.make_async_remote_copy(
            src_ref=y_buf.at[p], dst_ref=out.at[1, window], send_sem=y_send.at[p], recv_sem=y_recv.at[window],
            device_id={"tiles": before, "seg": p}, device_id_type=MESH,
        )

    def hand_across(window):
        return pltpu.make_async_remote_copy(
            src_ref=y_buf.at[1 - s], dst_ref=out.at[0, window], send_sem=y_send.at[2], recv_sem=y_recv.at[2],
            device_id={"seg": 1 - s}, device_id_type=MESH,
        )

    for p in range(2):
        for q in range(2):
            bins = slice(q * F + p * half, q * F + (p + 1) * half)
            y_buf[p, q] = jnp.transpose(spectra[bins] * gains).astype(jnp.bfloat16)

        @pl.when(t > 0)
        def _():
            hand_back(p, s).start()

    hand_across(s).start()
    keep = pltpu.make_async_copy(y_buf.at[s], out.at[0, s], out_sem.at[0])
    keep.start()

    @pl.when(t == tiles - 1)
    def _():
        blank[...] = jnp.zeros_like(blank)
        clear = pltpu.make_async_copy(blank, out.at[1], out_sem.at[1])
        clear.start()
        clear.wait()

    @pl.loop(1, tiles)
    def _(i):
        send(lax.rem(t + i, tiles)).wait_send()

    keep.wait()
    hand_across(1 - s).wait_recv()

    @pl.when(t < tiles - 1)
    def _():
        for window in range(2):
            hand_back(0, window).wait_recv()

    @pl.when(t > 0)
    def _():
        for p in range(2):
            hand_back(p, s).wait_send()

    hand_across(s).wait_send()


def whitened_spectra(records, channel_live, tiles):
    length = records.shape[1]
    group = channel_live.shape[0]
    half = F // 2
    analysis, synthesis = tables(tiles, length)
    in_hbm = pl.BlockSpec(memory_space=pltpu.HBM)
    return pl.pallas_call(
        functools.partial(spectra_kernel, tiles),
        out_shape=jax.ShapeDtypeStruct((2, 2, 2, group, half), jnp.bfloat16),
        in_specs=[in_hbm] * 4,
        out_specs=in_hbm,
        scratch_shapes=[
            pltpu.VMEM((tiles, length, group), jnp.bfloat16),
            pltpu.VMEM((2 * MODES + tiles, length), jnp.float32),
            pltpu.VMEM((2 * MODES, length), jnp.bfloat16),
            pltpu.VMEM((tiles // 2, 2 * F, 4 * MODES), jnp.bfloat16),
            pltpu.VMEM((1, group), jnp.int32),
            pltpu.VMEM((tiles, 2 * MODES, group), jnp.bfloat16),
            pltpu.VMEM((tiles * 2 * MODES, group), jnp.bfloat16),
            pltpu.VMEM((2 * F, group), jnp.float32),
            pltpu.VMEM((2, 2, group, half), jnp.bfloat16),
            pltpu.VMEM((2, 2, group, half), jnp.bfloat16),
            pltpu.SemaphoreType.DMA((tiles,)),
            pltpu.SemaphoreType.DMA,
            pltpu.SemaphoreType.DMA,
            pltpu.SemaphoreType.DMA,
            pltpu.SemaphoreType.DMA((2,)),
            pltpu.SemaphoreType.DMA((tiles,)),
            pltpu.SemaphoreType.DMA((tiles,)),
            pltpu.SemaphoreType.DMA((3,)),
            pltpu.SemaphoreType.DMA((3,)),
        ],
        compiler_params=pltpu.CompilerParams(
            collective_id=0, has_side_effects=True, vmem_limit_bytes=60 << 20
        ),
    )(records, jnp.asarray(analysis), jnp.asarray(synthesis), channel_live.reshape(1, group))


CHANNEL_BLOCK = 8
OFFSET_BLOCK = 32


def cross_kernel(scale, halves, out, wide, stack, sem):
    group = halves.shape[3]
    for w in range(2):
        for place in range(2):
            re, im = (halves[place, w, q].astype(jnp.float32) for q in range(2))
            rows = pl.ds(place * group, group)
            wide[w, 0, rows, :] = re
            wide[w, 1, rows, :] = im
            wide[w, 2, rows, :] = re + im

    def channel(c):
        (a0, b0), (a1, b1) = [[wide[w, q, pl.ds(c, 1), :] * scale for q in range(2)] for w in range(2)]
        pairs = ((2, b0, b1), (0, a0 - b0, a1 - b1), (1, a0 + b0, a1 + b1))
        for o in range(0, OFFS, OFFSET_BLOCK):
            rows = pl.ds(c + o, OFFSET_BLOCK)
            shared, more, less = (
                first * wide[0, q, rows, :] + second * wide[1, q, rows, :] for q, first, second in pairs
            )
            stack[0, c, pl.ds(o, OFFSET_BLOCK), :] = (shared + more).astype(jnp.bfloat16)
            stack[1, c, pl.ds(o, OFFSET_BLOCK), :] = (shared - less).astype(jnp.bfloat16)

    def copies(k):
        rows = pl.ds(k * CHANNEL_BLOCK, CHANNEL_BLOCK)
        return [pltpu.make_async_copy(stack.at[q, rows], out.at[q, rows], sem.at[q, k]) for q in range(2)]

    @pl.loop(0, group // CHANNEL_BLOCK)
    def _(k):
        for i in range(CHANNEL_BLOCK):
            channel(k * CHANNEL_BLOCK + i)
        for copy in copies(k):
            copy.start()

    @pl.loop(0, group // CHANNEL_BLOCK)
    def _(k):
        for copy in copies(k):
            copy.wait()


def cross_spectra(halves, windows):
    group, half = halves.shape[3:]
    return pl.pallas_call(
        functools.partial(cross_kernel, 1.0 / windows),
        out_shape=jax.ShapeDtypeStruct((2, group, OFFS, half), jnp.bfloat16),
        in_specs=[pl.BlockSpec(memory_space=pltpu.VMEM)],
        out_specs=pl.BlockSpec(memory_space=pltpu.HBM),
        scratch_shapes=[
            pltpu.VMEM((2, 3, 2 * group, half), jnp.float32),
            pltpu.VMEM((2, group, OFFS, half), jnp.bfloat16),
            pltpu.SemaphoreType.DMA((2, group // CHANNEL_BLOCK)),
        ],
        compiler_params=pltpu.CompilerParams(vmem_limit_bytes=60 << 20),
    )(halves)


def solution(mesh):
    tiles = mesh.shape["tiles"]

    def local(records, channel_live):
        halves = whitened_spectra(records, channel_live, tiles)
        return cross_spectra(halves, records.shape[0] * mesh.shape["seg"])

    in_specs = (P("seg", "tiles", "groups"), P(("groups", "tiles")))
    out_specs = P(None, ("groups", "tiles"), None, "seg")
    return jax.shard_map(local, mesh=mesh, in_specs=in_specs, out_specs=out_specs, check_vma=False)
```

```python
import functools
import math

import jax
import jax.numpy as jnp
import ml_dtypes
import numpy as np
from jax import lax
from jax.experimental import pallas as pl
from jax.experimental.pallas import tpu as pltpu
from jax.sharding import PartitionSpec as P

OFFS = 128
L = 12800
FIRST_BIN = 64
F = 256
MODES = 48
EPSILON = 1e-06
MESH = pl.DeviceIdType.MESH


def sequences(length):
    n = np.arange(length, dtype=np.float64)
    diagonal = ((length - 1 - 2 * n) / 2) ** 2 * np.cos(2 * np.pi * F / 2 / L)
    beside = n[1:] * (length - n[1:]) / 2
    matrix = np.diag(diagonal) + np.diag(beside, 1) + np.diag(beside, -1)
    rows = np.linalg.eigh(matrix)[1][:, ::-1][:, :MODES].T
    sign = np.sign(np.sum(rows * (1.0 + n / length + np.sin(n)), axis=1, keepdims=True))
    return rows * sign


def tables(tiles, length):
    rows = sequences(length)
    n = np.arange(length, dtype=np.float64) - (length - 1) / 2
    middle = FIRST_BIN + (F - 1) / 2
    turn = 2 * np.pi * middle * n / L
    taper = 0.5 - 0.5 * np.cos(2 * np.pi * np.arange(tiles * length) / L).reshape(tiles, length)
    modulated = np.concatenate([rows * np.cos(turn), -rows * np.sin(turn)])
    analysis = (np.round(np.concatenate([modulated, taper]) * 2.0**20) / 2.0**20).astype(np.float32)
    bins = np.arange(F, dtype=np.float64)
    spectrum = np.exp(-2j * np.pi * (bins[:, None] - (F - 1) / 2) * n / L) @ rows.T
    centre = np.arange(tiles) * length + (length - 1) / 2
    spectrum = spectrum * np.exp(-2j * np.pi * (bins + FIRST_BIN)[:, None] * centre[:, None, None] / L)
    re, im = spectrum.real, spectrum.imag
    whole = np.concatenate(
        [np.concatenate([re, -im], axis=2), np.concatenate([im, re], axis=2)], axis=1
    )
    pairs = np.concatenate([whole[0::2], whole[1::2]], axis=2)
    return analysis, pairs.astype(ml_dtypes.bfloat16)


def spectra_kernel(
    tiles, rec, analysis, synthesis, live, out,
    rec_buf, table, a_buf, s_buf, live_buf, send_buf, recv_buf, total, y_buf, blank,
    rec_sem, a_sem, s_sem, live_sem, out_sem, send_sem, recv_sem, y_send, y_recv,
):
    t, s = lax.axis_index("tiles"), lax.axis_index("seg")
    half = F // 2
    group = live.shape[1]

    def rec_copy(j):
        columns = pl.ds(pl.multiple_of(j * group, group), group)
        return pltpu.make_async_copy(rec.at[0, :, columns], rec_buf.at[j], rec_sem.at[j])

    def turn(i):
        m = lax.div(i, 2)
        return lax.rem(tiles + tiles // 2 + m - 2 * m * lax.rem(i, 2), tiles)

    a_copy = pltpu.make_async_copy(analysis, table, a_sem)
    a_copy.start()

    @pl.loop(1, tiles + 1)
    def _(i):
        rec_copy(lax.rem(t + turn(i), tiles)).start()

    s_copy = pltpu.make_async_copy(synthesis, s_buf, s_sem)
    s_copy.start()
    live_copy = pltpu.make_async_copy(live, live_buf, live_sem)
    live_copy.start()

    barrier = pltpu.get_barrier_semaphore()

    @pl.loop(1, tiles)
    def _(i):
        pl.semaphore_signal(barrier, inc=1, device_id={"tiles": lax.rem(t + i, tiles)}, device_id_type=MESH)

    for step in (0, 1, tiles - 1):
        pl.semaphore_signal(
            barrier, inc=1, device_id={"tiles": lax.rem(t + step, tiles), "seg": 1 - s}, device_id_type=MESH
        )

    def coefficients(j):
        rec_copy(j).wait()
        return jnp.dot(a_buf[...], rec_buf[j], preferred_element_type=jnp.float32).astype(jnp.bfloat16)

    def rows_of(j):
        return pl.ds(pl.multiple_of(j * 2 * MODES, 2 * MODES), 2 * MODES)

    def send(j):
        return pltpu.make_async_remote_copy(
            src_ref=send_buf.at[j], dst_ref=recv_buf.at[rows_of(t)], send_sem=send_sem.at[j],
            recv_sem=recv_sem.at[t], device_id={"tiles": j}, device_id_type=MESH,
        )

    def arrived(j):
        return pltpu.make_async_remote_copy(
            src_ref=send_buf.at[j], dst_ref=recv_buf.at[rows_of(j)], send_sem=send_sem.at[j],
            recv_sem=recv_sem.at[j], device_id={"tiles": j}, device_id_type=MESH,
        )

    a_copy.wait()
    taper = table[pl.ds(2 * MODES + t, 1), :]
    a_buf[...] = (table[pl.ds(0, 2 * MODES), :] * taper).astype(jnp.bfloat16)
    first = lax.rem(t + tiles // 2, tiles)
    send_buf[first] = coefficients(first)
    pl.semaphore_wait(barrier, tiles + 2)
    send(first).start()

    @pl.loop(2, tiles)
    def _(i):
        j = lax.rem(t + turn(i), tiles)
        send_buf[j] = coefficients(j)
        send(j).start()

    recv_buf[rows_of(t), :] = coefficients(t)
    s_copy.wait()

    def part(p):
        rows = pl.ds(pl.multiple_of(p * 4 * MODES, 4 * MODES), 4 * MODES)
        return jnp.dot(s_buf[p], recv_buf[rows, :], preferred_element_type=jnp.float32)

    pair, pairs = lax.div(t, 2), tiles // 2
    arrived(pair * 2 + 1 - lax.rem(t, 2)).wait_recv()
    total[...] = part(pair)

    @pl.loop(1, pairs)
    def _(i):
        p = lax.rem(pair + pairs - i, pairs)
        arrived(2 * p).wait_recv()
        arrived(2 * p + 1).wait_recv()
        total[...] += part(p)

    live_copy.wait()
    spectra = total[...]
    power = jnp.sum(spectra * spectra, axis=0, keepdims=True) * (1.0 / (2 * F))
    gains = lax.rsqrt(power + EPSILON) * live_buf[...].astype(jnp.float32)
    before = lax.rem(t + tiles - 1, tiles)

    def hand_back(p, window):
        return pltpu.make_async_remote_copy(
            src_ref=y_buf.at[p], dst_ref=out.at[1, window], send_sem=y_send.at[p], recv_sem=y_recv.at[window],
            device_id={"tiles": before, "seg": p}, device_id_type=MESH,
        )

    def hand_across(window):
        return pltpu.make_async_remote_copy(
            src_ref=y_buf.at[1 - s], dst_ref=out.at[0, window], send_sem=y_send.at[2], recv_sem=y_recv.at[2],
            device_id={"seg": 1 - s}, device_id_type=MESH,
        )

    for p in range(2):
        for q in range(2):
            bins = slice(q * F + p * half, q * F + (p + 1) * half)
            y_buf[p, q] = jnp.transpose(spectra[bins] * gains).astype(jnp.bfloat16)

        @pl.when(t > 0)
        def _():
            hand_back(p, s).start()

    hand_across(s).start()
    keep = pltpu.make_async_copy(y_buf.at[s], out.at[0, s], out_sem.at[0])
    keep.start()

    @pl.when(t == tiles - 1)
    def _():
        blank[...] = jnp.zeros_like(blank)
        clear = pltpu.make_async_copy(blank, out.at[1], out_sem.at[1])
        clear.start()
        clear.wait()

    @pl.loop(1, tiles)
    def _(i):
        send(lax.rem(t + i, tiles)).wait_send()

    keep.wait()
    hand_across(1 - s).wait_recv()

    @pl.when(t < tiles - 1)
    def _():
        for window in range(2):
            hand_back(0, window).wait_recv()

    @pl.when(t > 0)
    def _():
        for p in range(2):
            hand_back(p, s).wait_send()

    hand_across(s).wait_send()


def whitened_spectra(records, channel_live, tiles):
    length = records.shape[1]
    group = channel_live.shape[0]
    half = F // 2
    analysis, synthesis = tables(tiles, length)
    in_hbm = pl.BlockSpec(memory_space=pltpu.HBM)
    return pl.pallas_call(
        functools.partial(spectra_kernel, tiles),
        out_shape=jax.ShapeDtypeStruct((2, 2, 2, group, half), jnp.bfloat16),
        in_specs=[in_hbm] * 4,
        out_specs=pl.BlockSpec(memory_space=pl.ANY),
        scratch_shapes=[
            pltpu.VMEM((tiles, length, group), jnp.bfloat16),
            pltpu.VMEM((2 * MODES + tiles, length), jnp.float32),
            pltpu.VMEM((2 * MODES, length), jnp.bfloat16),
            pltpu.VMEM((tiles // 2, 2 * F, 4 * MODES), jnp.bfloat16),
            pltpu.VMEM((1, group), jnp.int32),
            pltpu.VMEM((tiles, 2 * MODES, group), jnp.bfloat16),
            pltpu.VMEM((tiles * 2 * MODES, group), jnp.bfloat16),
            pltpu.VMEM((2 * F, group), jnp.float32),
            pltpu.VMEM((2, 2, group, half), jnp.bfloat16),
            pltpu.VMEM((2, 2, group, half), jnp.bfloat16),
            pltpu.SemaphoreType.DMA((tiles,)),
            pltpu.SemaphoreType.DMA,
            pltpu.SemaphoreType.DMA,
            pltpu.SemaphoreType.DMA,
            pltpu.SemaphoreType.DMA((2,)),
            pltpu.SemaphoreType.DMA((tiles,)),
            pltpu.SemaphoreType.DMA((tiles,)),
            pltpu.SemaphoreType.DMA((3,)),
            pltpu.SemaphoreType.DMA((3,)),
        ],
        compiler_params=pltpu.CompilerParams(
            collective_id=0, has_side_effects=True, vmem_limit_bytes=214 << 18
        ),
    )(records, jnp.asarray(analysis), jnp.asarray(synthesis), channel_live.reshape(1, group))


CHANNEL_BLOCK = 8
OFFSET_BLOCK = 32


def cross_kernel(scale, halves, out, wide, stack, sem):
    group = halves.shape[3]
    for w in range(2):
        for place in range(2):
            re, im = (halves[place, w, q].astype(jnp.float32) for q in range(2))
            rows = pl.ds(place * group, group)
            wide[w, 0, rows, :] = re
            wide[w, 1, rows, :] = im
            wide[w, 2, rows, :] = re + im

    def channel(c):
        (a0, b0), (a1, b1) = [[wide[w, q, pl.ds(c, 1), :] * scale for q in range(2)] for w in range(2)]
        pairs = ((2, b0, b1), (0, a0 - b0, a1 - b1), (1, a0 + b0, a1 + b1))
        for o in range(0, OFFS, OFFSET_BLOCK):
            rows = pl.ds(c + o, OFFSET_BLOCK)
            shared, more, less = (
                first * wide[0, q, rows, :] + second * wide[1, q, rows, :] for q, first, second in pairs
            )
            stack[0, c, pl.ds(o, OFFSET_BLOCK), :] = (shared + more).astype(jnp.bfloat16)
            stack[1, c, pl.ds(o, OFFSET_BLOCK), :] = (shared - less).astype(jnp.bfloat16)

    def copies(k):
        rows = pl.ds(k * CHANNEL_BLOCK, CHANNEL_BLOCK)
        return [pltpu.make_async_copy(stack.at[q, rows], out.at[q, rows], sem.at[q, k]) for q in range(2)]

    @pl.loop(0, group // CHANNEL_BLOCK)
    def _(k):
        for i in range(CHANNEL_BLOCK):
            channel(k * CHANNEL_BLOCK + i)
        for copy in copies(k):
            copy.start()

    @pl.loop(0, group // CHANNEL_BLOCK)
    def _(k):
        for copy in copies(k):
            copy.wait()


def cross_spectra(halves, windows):
    group, half = halves.shape[3:]
    return pl.pallas_call(
        functools.partial(cross_kernel, 1.0 / windows),
        out_shape=jax.ShapeDtypeStruct((2, group, OFFS, half), jnp.bfloat16),
        in_specs=[pl.BlockSpec(memory_space=pltpu.VMEM)],
        out_specs=pl.BlockSpec(memory_space=pltpu.HBM),
        scratch_shapes=[
            pltpu.VMEM((2, 3, 2 * group, half), jnp.float32),
            pltpu.VMEM((2, group, OFFS, half), jnp.bfloat16),
            pltpu.SemaphoreType.DMA((2, group // CHANNEL_BLOCK)),
        ],
        compiler_params=pltpu.CompilerParams(vmem_limit_bytes=16 << 20),
    )(halves)


def solution(mesh):
    tiles = mesh.shape["tiles"]

    def local(records, channel_live):
        halves = whitened_spectra(records, channel_live, tiles)
        return cross_spectra(halves, records.shape[0] * mesh.shape["seg"])

    in_specs = (P("seg", "tiles", "groups"), P(("groups", "tiles")))
    out_specs = P(None, ("groups", "tiles"), None, "seg")
    return jax.shard_map(local, mesh=mesh, in_specs=in_specs, out_specs=out_specs, check_vma=False)
```
